32 devices in a mesh: track: 2 (over y), tm: 16 (over z, x, core).
Axes of the slice: x: 2, y: 2, z: 4, core: 2. Of those that a mesh axis runs over, the one named last changes fastest.
Arguments:
- track_query: bfloat16 [16, 2048, 1024], P('track', 'tm'), may hold values from -6 to 6
- track_key: bfloat16 [16, 2048, 1024], P('track', 'tm'), may hold values from -6 to 6
- track_value: bfloat16 [16, 2048, 1024], P('track', 'tm'), may hold values from -6 to 6
- log_decay: float32 [16, 8, 2048], P('track', None, 'tm'), may hold values from -2.3 to 0
- valid_length: int32 [16], replicated, may hold values from 512 to 2048, as said below
- initial_state: bfloat16 [16, 8, 128, 128], P('track'), may hold values from -24 to 24
- cross_query: bfloat16 [16, 2048, 1024], P('track', 'tm'), may hold values from -5 to 5
- cross_key: bfloat16 [16, 2048, 1024], P('track', 'tm'), may hold values from -5 to 5
- grad_out: bfloat16 [16, 2048, 1024], P('track', 'tm'), may hold values from -6 to 6
Outputs:
- grad_query: bfloat16 [16, 2048, 1024], P('track', 'tm')
- grad_key: bfloat16 [16, 2048, 1024], P('track', 'tm')
- grad_value: bfloat16 [16, 2048, 1024], P('track', 'tm')
- grad_cross_query: bfloat16 [16, 2048, 1024], P('track', 'tm')
- grad_cross_key: bfloat16 [16, 2048, 1024], P('track', 'tm')
The draws below stay inside these ranges and needn't reach their ends.
Inputs may be any that keep to these rules, and one draw needn't show every extreme that they name: `valid_length`: multiples of 128; one track has 2048 valid steps and one has exactly 512.
All inputs are finite; a program needn't handle non-finite values.
Results may differ from the reference program's by a relative error of at most 0.005.
Values may be sent and summed in bfloat16 or wider, within the bound.
A program may use at most 256 MiB of HBM per device.

```python
import jax
import jax.numpy as jnp
from jax import lax

H = 8
DH = 128
D = 1024
VOICE_PARTS = 16
SEQUENCE_LENGTH = 2048
SHORT = 512


def draw_valid_length(key, part):
    first_key, second_key = jax.random.split(jax.random.fold_in(key, 11))
    blocks = jax.random.randint(first_key, (VOICE_PARTS,), SHORT // 128, SEQUENCE_LENGTH // 128 + 1)
    lengths = blocks * 128
    picked = jax.random.permutation(second_key, VOICE_PARTS)
    lengths = lengths.at[picked[0]].set(SEQUENCE_LENGTH)
    lengths = lengths.at[picked[1]].set(SHORT)
    return lengths.astype(jnp.int32)


def draw_log_decay(key, part):
    gathered_lookup_vectors = jax.random.split(jax.random.fold_in(key, 23), 6)
    share_fast = 0.35
    chooser = jax.random.uniform(gathered_lookup_vectors[0], (VOICE_PARTS, H))
    fast_rate = jnp.exp(jax.random.uniform(gathered_lookup_vectors[1], (VOICE_PARTS, H), minval=jnp.log(1.0 / 50.0), maxval=jnp.log(1.0 / 30.0)))
    slow_rate = jnp.exp(jax.random.uniform(gathered_lookup_vectors[2], (VOICE_PARTS, H), minval=jnp.log(0.05 / SEQUENCE_LENGTH), maxval=jnp.log(0.5 / SEQUENCE_LENGTH)))
    head_rate = jnp.where(chooser < share_fast, fast_rate, slow_rate)
    roughness = jnp.exp(jax.random.uniform(gathered_lookup_vectors[3], (VOICE_PARTS, H, SEQUENCE_LENGTH), minval=jnp.log(0.5), maxval=jnp.log(2.0)))
    forget_gate_logarithm = -head_rate[:, :, None] * roughness
    moment_indices = jax.random.randint(gathered_lookup_vectors[4], (VOICE_PARTS, 3), 0, SEQUENCE_LENGTH)
    segment_length = jax.random.uniform(gathered_lookup_vectors[5], (VOICE_PARTS, 3), minval=0.22, maxval=0.69)
    segment_count = jnp.zeros((VOICE_PARTS, SEQUENCE_LENGTH), jnp.float32)
    segment_count = segment_count.at[jnp.arange(VOICE_PARTS)[:, None], moment_indices].add(segment_length)
    return (forget_gate_logarithm - segment_count[:, None, :]).astype(jnp.float32)


def cross_pair(key):
    gathered_lookup_vectors = jax.random.split(jax.random.fold_in(key, 37), 2)
    full_shape = (VOICE_PARTS, SEQUENCE_LENGTH, D)
    query_draw = jnp.clip(jax.random.normal(gathered_lookup_vectors[0], full_shape), -5.0, 5.0)
    key_draw = jnp.clip(jax.random.normal(gathered_lookup_vectors[1], full_shape), -5.0, 5.0)
    return (query_draw, key_draw)


def draw_cross_query(key, part):
    return cross_pair(key)[0].astype(jnp.bfloat16)


def draw_cross_key(key, part):
    return cross_pair(key)[1].astype(jnp.bfloat16)


def block_levels(own_key, extent, pieces, low, high):
    gain = 1.0
    for dim, shards_of in pieces:
        heights = jax.random.uniform(jax.random.fold_in(jax.random.fold_in(own_key, 6), dim), (shards_of,), jnp.float32, low / len(pieces), high / len(pieces))
        gain = gain * jnp.repeat(jnp.exp(heights), extent[dim] // shards_of).reshape((-1,) + (1,) * (len(extent) - 1 - dim))
    return gain


def centred(own_key, extent, deviation, reach, cuts=(), kind=jnp.bfloat16):
    entries = deviation * jax.random.normal(own_key, extent, jnp.float32)
    if cuts:
        entries = entries * block_levels(own_key, extent, cuts, -0.22, 0.18)
    return jnp.clip(entries, -reach, reach).astype(kind)


def setup_inputs(seed: int = 0) -> dict:
    streams_of = jax.random.split(jax.random.key(seed), 10)
    track_query = centred(streams_of[0], (VOICE_PARTS, SEQUENCE_LENGTH, D), 1.0, 6.0, ((0, 2), (1, 16)))
    track_key = centred(streams_of[1], (VOICE_PARTS, SEQUENCE_LENGTH, D), 1.0, 6.0, ((0, 2), (1, 16)))
    track_value = centred(streams_of[2], (VOICE_PARTS, SEQUENCE_LENGTH, D), 1.0, 6.0, ((0, 2), (1, 16)))
    log_decay = draw_log_decay(jax.random.fold_in(streams_of[9], 71), 0)
    valid_length = draw_valid_length(jax.random.fold_in(streams_of[9], 71), 0)
    initial_state = centred(streams_of[5], (VOICE_PARTS, H, DH, DH), 4.0, 24.0, ((0, 2),))
    cross_query = draw_cross_query(jax.random.fold_in(streams_of[9], 71), 0)
    cross_key = draw_cross_key(jax.random.fold_in(streams_of[9], 71), 0)
    grad_out = centred(streams_of[8], (VOICE_PARTS, SEQUENCE_LENGTH, D), 1.0, 6.0, ((0, 2), (1, 16)))
    return {"track_query": track_query, "track_key": track_key, "track_value": track_value, "log_decay": log_decay, "valid_length": valid_length, "initial_state": initial_state, "cross_query": cross_query, "cross_key": cross_key, "grad_out": grad_out}


EPSILON = 1e-06
HIGHEST_PRECISION = lax.Precision.HIGHEST
BLOCK_ROWS = 128

def track_forward(query_rows, key_rows, value_rows, decay_rows, valid_rows, start_state):
    head_count = decay_rows.shape[0]
    total_rows = query_rows.shape[0]
    model_width = query_rows.shape[1]
    head_size = model_width // head_count
    blocks = total_rows // BLOCK_ROWS
    split_shape = (blocks, BLOCK_ROWS, head_count, head_size)
    query_float = query_rows.astype(jnp.float32).reshape(split_shape)
    key_float = (key_rows.astype(jnp.float32) * valid_rows[:, None]).reshape(split_shape)
    value_float = value_rows.astype(jnp.float32).reshape(split_shape)
    decay_split = jnp.transpose(decay_rows.reshape(head_count, blocks, BLOCK_ROWS), (1, 0, 2))
    lower_mask = jnp.arange(BLOCK_ROWS)[:, None] >= jnp.arange(BLOCK_ROWS)[None, :]

    def block_step(carry_state, inputs):
        query_block, key_block, value_block, decay_block = inputs
        within = jnp.cumsum(decay_block, axis=-1)
        decay_matrix = jnp.exp(jnp.where(lower_mask, within[:, :, None] - within[:, None, :], -jnp.inf))
        scores = jnp.einsum('thc,shc->hts', query_block, key_block, precision=HIGHEST_PRECISION) * decay_matrix
        from_start = jnp.transpose(jnp.exp(within))[:, :, None]
        to_end = jnp.transpose(jnp.exp(within[:, -1:] - within))[:, :, None]
        outputs = jnp.einsum('hts,shd->thd', scores, value_block, precision=HIGHEST_PRECISION)
        outputs = outputs + from_start * jnp.einsum('thc,hcd->thd', query_block, carry_state, precision=HIGHEST_PRECISION)
        new_state = jnp.exp(within[:, -1])[:, None, None] * carry_state
        new_state = new_state + jnp.einsum('shc,shd->hcd', key_block * to_end, value_block, precision=HIGHEST_PRECISION)
        return (new_state, outputs)
    initial = start_state.astype(jnp.float32)
    _, outputs = lax.scan(block_step, initial, (query_float, key_float, value_float, decay_split))
    outputs = outputs.reshape(total_rows, head_count, head_size)
    mean_square = lax.optimization_barrier(jnp.mean(outputs * outputs, axis=-1, keepdims=True))
    normed = outputs * (1.0 / jnp.sqrt(mean_square + EPSILON)) * valid_rows[:, None, None]
    return normed.astype(jnp.bfloat16).reshape(total_rows, model_width)

def cross_mix(cross_query, cross_key, normed, valid_mask):
    query_float = cross_query.astype(jnp.float32).reshape(VOICE_PARTS, SEQUENCE_LENGTH, H, DH)
    key_float = cross_key.astype(jnp.float32).reshape(VOICE_PARTS, SEQUENCE_LENGTH, H, DH)
    normed_float = normed.astype(jnp.float32).reshape(VOICE_PARTS, SEQUENCE_LENGTH, H, DH)
    logits = jnp.einsum('ithc,jthc->thij', query_float, key_float, precision=HIGHEST_PRECISION) / float(DH) ** 0.5
    logits = jnp.where(jnp.transpose(valid_mask)[:, None, None, :] > 0, logits, -1e+30)
    weights = jax.nn.softmax(logits, axis=-1)
    mixed = jnp.einsum('thij,jthd->ithd', weights, normed_float, precision=HIGHEST_PRECISION)
    return (mixed * valid_mask[:, :, None, None]).reshape(VOICE_PARTS, SEQUENCE_LENGTH, D)

def reference(track_query, track_key, track_value, log_decay, valid_length, initial_state, cross_query, cross_key, grad_out):
    time_index = jnp.arange(SEQUENCE_LENGTH)
    valid_mask = (time_index[None, :] < valid_length[:, None]).astype(jnp.float32)
    normed = lax.map(lambda packed: track_forward(packed[0], packed[1], packed[2], packed[3], packed[4], packed[5]), (track_query, track_key, track_value, log_decay, valid_mask, initial_state))

    def cross_only(query_in, key_in, normed_in):
        return cross_mix(query_in, key_in, normed_in, valid_mask)
    _, pullback = jax.vjp(cross_only, cross_query, cross_key, normed)
    grad_cross_query, grad_cross_key, grad_normed = pullback(grad_out.astype(jnp.float32))

    def track_backward(packed):

        def forward(query_in, key_in, value_in):
            return track_forward(query_in, key_in, value_in, packed[3], packed[4], packed[6])
        _, track_pull = jax.vjp(forward, packed[0], packed[1], packed[2])
        return track_pull(packed[5])
    grad_query, grad_key, grad_value = lax.map(track_backward, (track_query, track_key, track_value, log_decay, valid_mask, grad_normed, initial_state))
    return (grad_query, grad_key, grad_value, grad_cross_query, grad_cross_key)
```

```python
import functools

import jax
import jax.numpy as jnp
from jax import lax
from jax.experimental import pallas as pl
from jax.experimental.pallas import tpu as pltpu
from jax.sharding import PartitionSpec as P

EPSILON = 1e-06
MESH = pl.DeviceIdType.MESH
BF = jnp.bfloat16
F32 = jnp.float32
TILE = 16
FAR = -1e30


def mm(a, b):
    return lax.dot_general(a, b, (((1,), (0,)), ((), ())), preferred_element_type=F32)


def mm_nt(a, b):
    return lax.dot_general(a, b, (((1,), (1,)), ((), ())), preferred_element_type=F32)


def mm_tn(a, b):
    return lax.dot_general(a, b, (((0,), (0,)), ((), ())), preferred_element_type=F32)


def remote(src, dst, send_sem, recv_sem, target):
    return pltpu.make_async_remote_copy(
        src_ref=src, dst_ref=dst, send_sem=send_sem, recv_sem=recv_sem,
        device_id=target, device_id_type=MESH,
    )


def split3(x):
    a = x.astype(BF)
    rest = x - a.astype(F32)
    b = rest.astype(BF)
    return a, b, (rest - b.astype(F32)).astype(BF)


def block_kernel(
    dims, len_ref, decay_ref, q_hbm, k_hbm, v_hbm, init_hbm, cq_hbm, ck_hbm, g_hbm,
    gq_ref, gk_ref, gv_ref, gcq_ref, gck_ref,
    q_ref, k_ref, v_ref, cq_ref, ck_ref, g_ref, init_ref,
    qo_ref, go_ref, part_send, part_recv, own_part,
    out_ref, norm_ref, state_ref, end_ref,
    sum_send, sum_recv, plane_send, plane_recv, start_send,
    e_ref, p_ref, bias_ref, gn_ref, col_ref, row_ref, ratio_ref,
    stat_own, stat_in, total_ref, dec_in, dec_plane,
    in_sem, y_send, y_recv, s_send, s_recv, r_send, r_recv,
    a_send, a_recv, b_send, b_recv, c_send, c_recv, d_send, d_recv, h_send, h_recv,
):
    groups, count, plane, heads = dims
    planes = count // plane
    tracks, rows, width = q_ref.shape
    size = width // heads
    own = tracks // plane
    tiles = rows // TILE
    span = tracks * TILE
    lanes = groups * span
    scale = 1.0 / float(size) ** 0.5
    pair = 2 if tracks % 2 == 0 else 1

    me = lax.axis_index("tm")
    mine = lax.axis_index("track")
    p = lax.rem(me, plane)
    z = me // plane
    time_first = me * rows

    def cut(h):
        return slice(h * size, (h + 1) * size)

    def plane_peer(r):
        return lax.rem(p + r, plane)

    def plane_id(peer):
        return {"tm": z * plane + peer}

    def track_id(s):
        return {"track": lax.rem(mine + s, groups)}

    hbm = (k_hbm, v_hbm, q_hbm, init_hbm.at[pl.ds(p * own, own)], ck_hbm, cq_hbm, g_hbm)
    vmem = (k_ref, v_ref, q_ref, init_ref, ck_ref, cq_ref, g_ref)
    loads = [pltpu.make_async_copy(a, b, in_sem.at[i]) for i, (a, b) in enumerate(zip(hbm, vmem))]
    for load in loads:
        load.start()

    barrier = pltpu.get_barrier_semaphore()
    for r in range(1, plane):
        pl.semaphore_signal(barrier, inc=1, device_id=plane_id(plane_peer(r)), device_id_type=MESH)
    for r in range(1, planes):
        other = lax.rem(z + r, planes) * plane + p
        pl.semaphore_signal(barrier, inc=1, device_id={"tm": other}, device_id_type=MESH)
    for s in range(1, groups):
        pl.semaphore_signal(barrier, inc=1, device_id=track_id(s), device_id_type=MESH)
    pl.semaphore_wait(barrier, plane - 1 + planes - 1 + groups - 1)

    def y_copies(h):
        return [
            remote(
                src.at[:, :, cut(h)], dst.at[s - 1, :, :, cut(h)],
                y_send.at[kind, h, s - 1], y_recv.at[kind, h, s - 1], track_id(s),
            )
            for s in range(1, groups)
            for kind, (src, dst) in enumerate(((cq_hbm, qo_ref), (g_hbm, go_ref)))
        ]

    def start_y(h):
        if h < heads:
            for copy in y_copies(h):
                copy.start()

    start_y(0)
    start_y(1)

    t_index = lax.broadcasted_iota(jnp.int32, (rows, rows), 0)
    s_index = lax.broadcasted_iota(jnp.int32, (rows, rows), 1)
    lower_mask = t_index >= s_index
    upper_mask = t_index <= s_index
    lower = jnp.where(lower_mask, 1.0, 0.0).astype(BF)
    upper = jnp.where(upper_mask, 1.0, 0.0).astype(BF)
    row_time = time_first + lax.broadcasted_iota(jnp.int32, (rows, 1), 0)

    for x in range(tracks):
        parts = split3(decay_ref[x])
        col = sum(mm_nt(lower, part) for part in parts)
        row = sum(mm(part, upper) for part in parts)
        valid = jnp.where(row_time < len_ref[mine * tracks + x], 1.0, 0.0)
        col_ref[x, :, 0:heads] = col
        col_ref[x, :, heads : 2 * heads] = jnp.exp(col)
        col_ref[x, :, 2 * heads : 3 * heads] = jnp.exp(col[rows - 1 : rows, :] - col) * valid
        col_ref[x, :, 3 * heads : 3 * heads + 1] = valid
        row_ref[x] = row
        total = jnp.broadcast_to(jnp.exp(row[:, rows - 1 : rows]), (heads, 128))
        for h in range(heads):
            at = h * own + x % own
            total_ref[x // own, at : at + 1, :] = total[h : h + 1]

    def d_copy(r):
        peer = plane_peer(r)
        return remote(
            total_ref.at[peer], dec_in.at[p], d_send.at[r - 1], d_recv.at[r - 1], plane_id(peer)
        )

    for r in range(1, plane):
        d_copy(r).start()
    dec_in[p] = total_ref[p]

    def within(x, h):
        return col_ref[x, :, h : h + 1]

    def from_start(x, h):
        return col_ref[x, :, heads + h : heads + h + 1]

    def to_end(x, h):
        return col_ref[x, :, 2 * heads + h : 2 * heads + h + 1]

    def valid_col(x):
        return col_ref[x, :, 3 * heads : 3 * heads + 1]

    def each_track(body, step=pair):
        def run(i, carry):
            for j in range(step):
                body(i * step + j)
            return carry

        lax.fori_loop(0, tracks // step, run, 0)

    def a_copy(d, h, r):
        peer = plane_peer(r)
        return remote(
            sum_send.at[h, pl.ds(peer * own, own)], sum_recv.at[d, h, p],
            a_send.at[d, h, r - 1], a_recv.at[d, h, r - 1], plane_id(peer),
        )

    def send_sums(d, h):
        for r in range(1, plane):
            a_copy(d, h, r).start()
        sum_recv[d, h, p] = sum_send[h, pl.ds(p * own, own)]

    def b_copy(d, h, r):
        target = lax.rem(z + (r if d == 0 else planes - r), planes)
        return remote(
            plane_send.at[d, h], plane_recv.at[h, z],
            b_send.at[d, h, r - 1], b_recv.at[d, h, r - 1], {"tm": target * plane + p},
        )

    def sends_plane(d, r):
        return z + r < planes if d == 0 else z - r >= 0

    def takes_plane(d, r):
        return sends_plane(1 - d, r)

    def order(d):
        return range(plane) if d == 0 else range(plane - 1, -1, -1)

    def plane_total(d, h):
        for r in range(1, plane):
            a_copy(d, h, r).wait_recv()
        for x in range(own):
            at = h * own + x
            carry = None
            for src in order(d):
                term = sum_recv[d, h, src, x].astype(F32)
                carry = term if carry is None else dec_in[src, at : at + 1, :] * carry + term
            plane_send[d, h, x] = carry.astype(BF)
        for r in range(1, planes):
            @pl.when(sends_plane(d, r))
            def _():
                b_copy(d, h, r).start()

    def c_copy(d, h, r):
        peer = plane_peer(r)
        dst = state_ref if d == 0 else end_ref
        return remote(
            start_send.at[h, peer], dst.at[h, pl.ds(p * own, own)],
            c_send.at[d, h, r - 1], c_recv.at[d, h, r - 1], plane_id(peer),
        )

    def send_states(d, h):
        for r in range(1, planes):
            @pl.when(takes_plane(d, r))
            def _():
                b_copy(d, h, r).wait_recv()
        for x in range(own):
            at = h * own + x

            def earlier(i, carry):
                src = i if d == 0 else planes - 1 - i
                return dec_plane[src, at : at + 1, :] * carry + plane_recv[h, src, x].astype(F32)

            carry = init_ref[x, h].astype(F32) if d == 0 else jnp.zeros((size, size), F32)
            carry = lax.fori_loop(0, z if d == 0 else planes - 1 - z, earlier, carry)
            for n, src in enumerate(order(d)):
                start_send[h, src, x] = carry.astype(BF)
                if n < plane - 1:
                    carry = dec_in[src, at : at + 1, :] * carry + sum_recv[d, h, src, x].astype(F32)
        for r in range(1, plane):
            c_copy(d, h, r).start()
        dst = state_ref if d == 0 else end_ref
        dst[h, pl.ds(p * own, own)] = start_send[h, p]

    def wait_states(d, h):
        for r in range(1, plane):
            c_copy(d, h, r).wait_recv()

    def drain_scan(d):
        for h in range(heads):
            for r in range(1, plane):
                a_copy(d, h, r).wait_send()
                c_copy(d, h, r).wait_send()
            for r in range(1, planes):
                @pl.when(sends_plane(d, r))
                def _():
                    b_copy(d, h, r).wait_send()

    def forward_sums(h):
        def body(x):
            key = (k_ref[x, :, cut(h)].astype(F32) * to_end(x, h)).astype(BF)
            sum_send[h, x] = mm_tn(key, v_ref[x, :, cut(h)]).astype(BF)

        each_track(body)
        send_sums(0, h)

    def forward_rows(h):
        wait_states(0, h)

        def body(x):
            q = q_ref[x, :, cut(h)]
            valid = valid_col(x)
            key = (k_ref[x, :, cut(h)].astype(F32) * valid).astype(BF)
            decay = jnp.exp(jnp.where(lower_mask, within(x, h) - row_ref[x, h : h + 1, :], FAR))
            scores = (mm_nt(q, key) * decay).astype(BF)
            outputs = mm(scores, v_ref[x, :, cut(h)]) + from_start(x, h) * mm(q, state_ref[h, x])
            square = jnp.mean(outputs * outputs, axis=-1, keepdims=True)
            inverse = lax.rsqrt(square + EPSILON) * valid
            norm_ref[x, :, cut(h)] = (outputs * inverse).astype(BF)
            out_ref[x, :, cut(h)] = outputs.astype(BF)

        each_track(body)

    def backward_sums(h):
        def body(x):
            outputs = out_ref[x, :, cut(h)].astype(F32)
            square = jnp.mean(outputs * outputs, axis=-1, keepdims=True)
            inverse = lax.rsqrt(square + EPSILON)
            unit = outputs * inverse
            grad = gn_ref[x]
            along = jnp.mean(grad * unit, axis=-1, keepdims=True)
            grad = ((inverse * valid_col(x)) * (grad - unit * along)).astype(BF)
            out_ref[x, :, cut(h)] = grad
            q_from = (q_ref[x, :, cut(h)].astype(F32) * from_start(x, h)).astype(BF)
            sum_send[h, x] = mm_tn(q_from, grad).astype(BF)

        each_track(body)
        send_sums(1, h)

    def backward_rows(h):
        wait_states(1, h)

        def body(x):
            q = q_ref[x, :, cut(h)]
            v = v_ref[x, :, cut(h)]
            valid = valid_col(x)
            key = (k_ref[x, :, cut(h)].astype(F32) * valid).astype(BF)
            grad = out_ref[x, :, cut(h)]
            end_grad = end_ref[h, x]
            decay = jnp.exp(jnp.where(upper_mask, row_ref[x, h : h + 1, :] - within(x, h), FAR))
            grad_scores = (mm_nt(v, grad) * decay).astype(BF)
            scores = (mm_nt(key, q) * decay).astype(BF)
            grad_query = mm_tn(grad_scores, key)
            grad_query = grad_query + from_start(x, h) * mm_nt(grad, state_ref[h, x])
            gq_ref[x, :, cut(h)] = grad_query.astype(BF)
            late = to_end(x, h)
            grad_key = valid * mm(grad_scores, q) + late * mm_nt(v, end_grad)
            gk_ref[x, :, cut(h)] = grad_key.astype(BF)
            grad_value = mm(scores, grad) + late * mm(key, end_grad)
            gv_ref[x, :, cut(h)] = grad_value.astype(BF)

        each_track(body)

    def shared_tables():
        row = lax.broadcasted_iota(jnp.int32, (span, 1), 0)
        lane = lax.broadcasted_iota(jnp.int32, (1, lanes), 1)
        key_length = jnp.zeros((span, 1), jnp.int32)
        for x in range(tracks):
            inside = (row >= x * TILE) & (row < (x + 1) * TILE)
            key_length = jnp.where(inside, len_ref[mine * tracks + x], key_length)
        query_length = jnp.zeros((1, lanes), jnp.int32)
        for s in range(groups):
            group = lax.rem(mine + groups - s, groups)
            for x in range(tracks):
                first = (s * tracks + x) * TILE
                inside = (lane >= first) & (lane < first + TILE)
                query_length = jnp.where(inside, len_ref[group * tracks + x], query_length)
        row_in, lane_in = lax.rem(row, TILE), lax.rem(lane, TILE)
        same = row_in == lane_in
        for tile in range(tiles):
            first = time_first + tile * TILE
            bias_ref[tile] = jnp.where(same & (first + row_in < key_length), 0.0, FAR)
            ratio_ref[2, tile : tile + 1, :] = jnp.where(first + lane_in < query_length, 1.0, 0.0)

    def gather(own_ref, other_ref, at, h):
        pieces = [own_ref[:, at, cut(h)].reshape(span, size)]
        pieces += [other_ref[s, :, at, cut(h)].reshape(span, size) for s in range(groups - 1)]
        return jnp.concatenate(pieces, axis=0)

    def each_tile(body):
        step = 2 if tiles % 2 == 0 else 1

        def run(i, carry):
            for j in range(step):
                tile = i * step + j
                body(tile, pl.ds(pl.multiple_of(tile * TILE, TILE), TILE))
            return carry

        lax.fori_loop(0, tiles // step, run, 0)

    def s_copy(h, s):
        return remote(
            stat_own.at[h], stat_in.at[s - 1, h], s_send.at[h, s - 1], s_recv.at[h, s - 1],
            track_id(s),
        )

    def cross_logits(h):
        for copy in y_copies(h):
            copy.wait_recv()
        slot = h % 2

        def body(tile, at):
            key = ck_ref[:, at, cut(h)].reshape(span, size)
            normed = norm_ref[:, at, cut(h)].reshape(span, size)
            logits = mm_nt(key, gather(cq_ref, qo_ref, at, h)) * scale + bias_ref[tile]
            top = jnp.max(logits, axis=0, keepdims=True)
            e = jnp.exp(logits - top)
            product = mm_nt(normed, gather(g_ref, go_ref, at, h))
            e_ref[slot, tile] = e
            p_ref[slot, tile] = product
            stat_own[h, 0, pl.ds(tile, 1), :] = top
            stat_own[h, 1, pl.ds(tile, 1), :] = jnp.sum(e, axis=0, keepdims=True)
            stat_own[h, 2, pl.ds(tile, 1), :] = jnp.sum(e * product, axis=0, keepdims=True)

        each_tile(body)
        for s in range(1, groups):
            s_copy(h, s).start()

    def p_copy(h, s):
        back = groups - s
        return remote(
            part_send.at[s - 1, :, :, cut(h)], part_recv.at[back - 1, :, :, cut(h)],
            r_send.at[h, s - 1], r_recv.at[h, back - 1],
            {"track": lax.rem(mine + groups - s, groups)},
        )

    def cross_grads(h):
        for s in range(1, groups):
            s_copy(h, s).wait_recv()
        slot = h % 2
        stats = [[stat_own[h, i] for i in range(3)]]
        for s in range(1, groups):
            away = (groups - s) * span
            pieces = [stat_in[s - 1, h, i] for i in range(3)]
            stats.append([jnp.concatenate([a[:, away:], a[:, :away]], axis=1) for a in pieces])
        top = functools.reduce(jnp.maximum, [a[0] for a in stats])
        weights = [jnp.exp(a[0] - top) for a in stats]
        inverse = 1.0 / sum(w * a[1] for w, a in zip(weights, stats))
        ratio_ref[0] = weights[0] * inverse * ratio_ref[2]
        ratio_ref[1] = sum(w * a[2] for w, a in zip(weights, stats)) * inverse

        def body(tile, at):
            key = ck_ref[:, at, cut(h)].reshape(span, size)
            cotangent = gather(g_ref, go_ref, at, h)
            w = e_ref[slot, tile] * ratio_ref[0, pl.ds(tile, 1), :]
            high = w.astype(BF)
            low = (w - high.astype(F32)).astype(BF)
            gn_ref[:, at, :] = (mm(high, cotangent) + mm(low, cotangent)).reshape(
                tracks, TILE, size
            )
            grad = w * ((p_ref[slot, tile] - ratio_ref[1, pl.ds(tile, 1), :]) * scale)
            grad = grad.astype(BF)
            query = gather(cq_ref, qo_ref, at, h)
            gck_ref[:, at, cut(h)] = mm(grad, query).astype(BF).reshape(tracks, TILE, size)
            parts = mm_tn(grad, key)
            own_part[:, at, cut(h)] = parts[:span].reshape(tracks, TILE, size)
            for s in range(1, groups):
                piece = parts[s * span : (s + 1) * span].astype(BF)
                part_send[s - 1, :, at, cut(h)] = piece.reshape(tracks, TILE, size)

        each_tile(body)

    def start_parts(h):
        for s in range(1, groups):
            p_copy(h, s).start()

    def add_parts(h):
        for s in range(1, groups):
            p_copy(h, s).wait_recv()

        def body(x):
            value = own_part[x, :, cut(h)]
            for s in range(groups - 1):
                value = value + part_recv[s, x, :, cut(h)].astype(F32)
            gcq_ref[x, :, cut(h)] = value.astype(BF)

        each_track(body)

    loads[0].wait()
    loads[1].wait()
    for h in range(heads):
        forward_sums(h)
    for r in range(1, plane):
        d_copy(r).wait_recv()
    whole = dec_in[0]
    for src in range(1, plane):
        whole = whole * dec_in[src]
    dec_plane[z] = whole

    def h_copy(r):
        other = lax.rem(z + r, planes) * plane + p
        return remote(
            dec_plane.at[z], dec_plane.at[z], h_send.at[r - 1], h_recv.at[r - 1], {"tm": other}
        )

    for r in range(1, planes):
        h_copy(r).start()
    start_y(2)
    shared_tables()
    loads[2].wait()
    loads[3].wait()
    for i in range(heads + 2):
        if i < heads:
            plane_total(0, i)
        if i == 0:
            for r in range(1, planes):
                h_copy(r).wait_recv()
        if 1 <= i <= heads:
            send_states(0, i - 1)
        if i >= 2:
            forward_rows(i - 2)
        if i == 4:
            start_y(3)
        if i == 7:
            start_y(4)
    for i in (4, 5, 6):
        loads[i].wait()
    drain_scan(0)

    cross_logits(0)
    for i in range(heads + 4):
        if i + 1 < heads:
            cross_logits(i + 1)
        if i < heads:
            if i == 0:
                start_y(5)
            if i == 2:
                start_y(6)
            if i == 3:
                start_y(7)
            if heads > 8 and i >= 3:
                start_y(i + 5)
            cross_grads(i)
            if i + 1 >= heads - 1:
                for h in range(heads):
                    if h == i or (i + 1 == heads - 1 and h < i):
                        start_parts(h)
            backward_sums(i)
        if 1 <= i <= heads:
            plane_total(1, i - 1)
        if 2 <= i <= heads + 1:
            send_states(1, i - 2)
        if 4 <= i:
            backward_rows(i - 4)
    for h in range(heads):
        add_parts(h)

    drain_scan(1)
    for r in range(1, plane):
        d_copy(r).wait_send()
    for r in range(1, planes):
        h_copy(r).wait_send()
    for h in range(heads):
        for copy in y_copies(h):
            copy.wait_send()
        for s in range(1, groups):
            s_copy(h, s).wait_send()
            p_copy(h, s).wait_send()


def per_device(
    count,
    groups,
    track_query,
    track_key,
    track_value,
    log_decay,
    valid_length,
    initial_state,
    cross_query,
    cross_key,
    grad_out,
):
    tracks, rows, width = track_query.shape
    heads = log_decay.shape[1]
    size = width // heads
    plane = max(n for n in (4, 2, 1) if tracks % n == 0 and count % n == 0)
    planes = count // plane
    own = tracks // plane
    tiles = rows // TILE
    span = tracks * TILE
    lanes = groups * span
    others = max(groups - 1, 1)
    peers = max(plane - 1, 1)
    layers = max(planes - 1, 1)
    vmem = pl.BlockSpec(memory_space=pltpu.VMEM)
    anywhere = pl.BlockSpec(memory_space=pl.ANY)
    wide = jax.ShapeDtypeStruct((tracks, rows, width), BF)
    block = pltpu.VMEM((tracks, rows, width), BF)
    blocks = pltpu.VMEM((others, tracks, rows, width), BF)
    states = pltpu.VMEM((heads, tracks, size, size), BF)
    dma = pltpu.SemaphoreType.DMA
    dot_flops = 2 * tracks * heads * rows * size * size
    return pl.pallas_call(
        functools.partial(block_kernel, (groups, count, plane, heads)),
        out_shape=(wide,) * 5,
        in_specs=[pl.BlockSpec(memory_space=pltpu.SMEM), vmem] + [anywhere] * 7,
        out_specs=(vmem,) * 5,
        scratch_shapes=[block] * 6
        + [pltpu.VMEM((own, heads, size, size), BF)]
        + [blocks] * 4
        + [pltpu.VMEM((tracks, rows, width), F32), block, block, states, states]
        + [
            states,
            pltpu.VMEM((2, heads, plane, own, size, size), BF),
            pltpu.VMEM((2, heads, own, size, size), BF),
            pltpu.VMEM((heads, planes, own, size, size), BF),
            pltpu.VMEM((heads, plane, own, size, size), BF),
            pltpu.VMEM((2, tiles, span, lanes), F32),
            pltpu.VMEM((2, tiles, span, lanes), F32),
            pltpu.VMEM((tiles, span, lanes), F32),
            pltpu.VMEM((tracks, rows, size), F32),
            pltpu.VMEM((tracks, rows, 128), F32),
            pltpu.VMEM((tracks, heads, rows), F32),
            pltpu.VMEM((3, tiles, lanes), F32),
            pltpu.VMEM((heads, 3, tiles, lanes), F32),
            pltpu.VMEM((others, heads, 3, tiles, lanes), F32),
            pltpu.VMEM((plane, heads * own, 128), F32),
            pltpu.VMEM((plane, heads * own, 128), F32),
            pltpu.VMEM((planes, heads * own, 128), F32),
            dma((7,)),
            dma((2, heads, others)),
            dma((2, heads, others)),
        ]
        + [dma((heads, others))] * 4
        + [dma((2, heads, peers))] * 2
        + [dma((2, heads, layers))] * 2
        + [dma((2, heads, peers))] * 2
        + [dma((peers,))] * 2
        + [dma((layers,))] * 2,
        compiler_params=pltpu.CompilerParams(
            collective_id=0, has_side_effects=True, vmem_limit_bytes=67043328
        ),
        cost_estimate=pl.CostEstimate(
            flops=20 * dot_flops, bytes_accessed=24 * tracks * rows * width, transcendentals=0
        ),
        name="block_backward",
    )(
        valid_length, log_decay, track_query, track_key, track_value, initial_state,
        cross_query, cross_key, grad_out,
    )


def solution(mesh):
    wide = P("track", "tm", None)
    return jax.shard_map(
        functools.partial(per_device, mesh.shape["tm"], mesh.shape["track"]),
        mesh=mesh,
        in_specs=(
            wide,
            wide,
            wide,
            P("track", None, "tm"),
            P(),
            P("track", None, None, None),
            wide,
            wide,
            wide,
        ),
        out_specs=(wide,) * 5,
        check_vma=False,
    )
```

```python
import functools

import jax
import jax.numpy as jnp
from jax import lax
from jax.experimental import pallas as pl
from jax.experimental.pallas import tpu as pltpu
from jax.sharding import PartitionSpec as P

EPSILON = 1e-06
MESH = pl.DeviceIdType.MESH
BF = jnp.bfloat16
F32 = jnp.float32
TILE = 16
VMEM_BYTES = 67043328
FAR = -1e30


def mm(a, b):
    return lax.dot_general(a, b, (((1,), (0,)), ((), ())), preferred_element_type=F32)


def mm_nt(a, b):
    return lax.dot_general(a, b, (((1,), (1,)), ((), ())), preferred_element_type=F32)


def mm_tn(a, b):
    return lax.dot_general(a, b, (((0,), (0,)), ((), ())), preferred_element_type=F32)


def remote(src, dst, send_sem, recv_sem, target):
    return pltpu.make_async_remote_copy(
        src_ref=src, dst_ref=dst, send_sem=send_sem, recv_sem=recv_sem,
        device_id=target, device_id_type=MESH,
    )


def split3(x):
    a = x.astype(BF)
    rest = x - a.astype(F32)
    b = rest.astype(BF)
    return a, b, (rest - b.astype(F32)).astype(BF)


def block_kernel(
    dims, len_ref, decay_ref, q_hbm, k_hbm, v_hbm, init_hbm, cq_hbm, ck_hbm, g_hbm,
    gq_ref, gk_ref, gv_ref, gcq_ref, gck_ref,
    q_ref, k_ref, v_ref, cq_ref, ck_ref, g_ref, init_ref,
    qo_ref, go_ref, part_send, part_recv, own_part,
    out_ref, norm_ref, state_ref, end_ref,
    sum_send, core_recv, chip_send, chip_own, chip_recv, relay_send, relay_recv,
    x_start, chip_start, core_start,
    e_ref, p_ref, bias_ref, gn_ref, col_ref, row_ref, ratio_ref,
    stat_own, stat_in, total_ref, core_total, chip_total, factor_ref,
    in_sem, y_send, y_recv, s_send, s_recv, r_send, r_recv, scan_send, scan_recv, d_send, d_recv,
):
    groups, count, cores, chips, heads = dims
    planes = count // (cores * chips)
    tracks, rows, width = q_ref.shape
    size = width // heads
    half = tracks // cores
    own = half // chips
    tiles = rows // TILE
    span = tracks * TILE
    lanes = groups * span
    scale = 1.0 / float(size) ** 0.5
    pair = 2 if tracks % 2 == 0 else 1

    me = lax.axis_index("tm")
    mine = lax.axis_index("track")
    c = lax.rem(me, cores)
    chip = lax.rem(me // cores, chips)
    z = me // (cores * chips)
    mine_first = c * half + chip * own
    time_first = me * rows

    def cut(h):
        return slice(h * size, (h + 1) * size)

    def place(plane, column, core):
        return {"tm": (plane * chips + column) * cores + core}

    core_id = place(z, chip, lax.rem(c + 1, cores))
    chip_id = place(z, lax.rem(chip + 1, chips), c)

    def relay_id(d):
        return place(lax.rem(z + (1 if d == 0 else planes - 1), planes), chip, c)

    def first_plane(d):
        return z == (0 if d == 0 else planes - 1)

    def track_id(s):
        return {"track": lax.rem(mine + s, groups)}

    hbm = (k_hbm, v_hbm, q_hbm, init_hbm.at[pl.ds(mine_first, own)], ck_hbm, cq_hbm, g_hbm)
    vmem = (k_ref, v_ref, q_ref, init_ref, ck_ref, cq_ref, g_ref)
    loads = [pltpu.make_async_copy(a, b, in_sem.at[i]) for i, (a, b) in enumerate(zip(hbm, vmem))]
    for load in loads:
        load.start()

    barrier = pltpu.get_barrier_semaphore()
    peers = [track_id(s) for s in range(1, groups)]
    if cores > 1:
        peers.append(core_id)
    if chips > 1:
        peers.append(chip_id)
    for peer in peers:
        pl.semaphore_signal(barrier, inc=1, device_id=peer, device_id_type=MESH)
    for d in range(2):
        @pl.when(jnp.logical_not(first_plane(1 - d)))
        def _():
            pl.semaphore_signal(barrier, inc=1, device_id=relay_id(d), device_id_type=MESH)
    inner = jnp.where(first_plane(0), 0, 1) + jnp.where(first_plane(1), 0, 1)
    pl.semaphore_wait(barrier, len(peers) + inner)

    def y_copies(h):
        return [
            remote(
                src.at[:, :, cut(h)], dst.at[s - 1, :, :, cut(h)],
                y_send.at[kind, h, s - 1], y_recv.at[kind, h, s - 1], track_id(s),
            )
            for s in range(1, groups)
            for kind, (src, dst) in enumerate(((cq_hbm, qo_ref), (g_hbm, go_ref)))
        ]

    def start_y(h):
        if h < heads:
            for copy in y_copies(h):
                copy.start()

    for h in range(4):
        start_y(h)

    t_index = lax.broadcasted_iota(jnp.int32, (rows, rows), 0)
    s_index = lax.broadcasted_iota(jnp.int32, (rows, rows), 1)
    lower_mask = t_index >= s_index
    upper_mask = t_index <= s_index
    lower = jnp.where(lower_mask, 1.0, 0.0).astype(BF)
    upper = jnp.where(upper_mask, 1.0, 0.0).astype(BF)
    row_time = time_first + lax.broadcasted_iota(jnp.int32, (rows, 1), 0)

    for x in range(tracks):
        parts = split3(decay_ref[x])
        col = sum(mm_nt(lower, part) for part in parts)
        row = sum(mm(part, upper) for part in parts)
        valid = jnp.where(row_time < len_ref[mine * tracks + x], 1.0, 0.0)
        col_ref[x, :, 0:heads] = col
        col_ref[x, :, heads : 2 * heads] = jnp.exp(col)
        col_ref[x, :, 2 * heads : 3 * heads] = jnp.exp(col[rows - 1 : rows, :] - col) * valid
        col_ref[x, :, 3 * heads : 3 * heads + 1] = valid
        row_ref[x] = row
        total = jnp.broadcast_to(jnp.exp(row[:, rows - 1 : rows]), (heads, 128))
        for h in range(heads):
            at = h * half + x % half
            total_ref[x // half, at : at + 1, :] = total[h : h + 1]

    def d_copy(level):
        if level == 0:
            other = lax.rem(c + 1, cores)
            return remote(total_ref.at[other], core_total, d_send.at[0], d_recv.at[0], core_id)
        return remote(chip_total.at[0], chip_total.at[1], d_send.at[1], d_recv.at[1], chip_id)

    if cores > 1:
        d_copy(0).start()

    def within(x, h):
        return col_ref[x, :, h : h + 1]

    def from_start(x, h):
        return col_ref[x, :, heads + h : heads + h + 1]

    def to_end(x, h):
        return col_ref[x, :, 2 * heads + h : 2 * heads + h + 1]

    def valid_col(x):
        return col_ref[x, :, 3 * heads : 3 * heads + 1]

    def each_track(body, step=pair):
        def run(i, carry):
            for j in range(step):
                body(i * step + j)
            return carry

        lax.fori_loop(0, tracks // step, run, 0)

    def level_factors(level, earlier, own_decay, other_decay):
        for d in range(2):
            first = earlier(d)
            one, none = jnp.ones_like(own_decay), jnp.zeros_like(own_decay)
            factor_ref[level, d, 0] = jnp.where(first, other_decay, one)
            factor_ref[level, d, 1] = jnp.where(first, one, own_decay)
            factor_ref[level, d, 2] = jnp.where(first, one, other_decay)
            factor_ref[level, d, 3] = jnp.where(first, none, one)
            factor_ref[level, d, 4] = jnp.where(first, own_decay, one)
            factor_ref[level, d, 5] = jnp.where(first, one, none)

    def core_factors():
        own_decay = total_ref[c]
        whole = own_decay
        if cores > 1:
            d_copy(0).wait_recv()
            other_decay = core_total[...]
            whole = own_decay * other_decay
            level_factors(0, lambda d: c == (0 if d == 0 else 1), own_decay, other_decay)
        chip_total[0] = whole
        if chips > 1:
            d_copy(1).start()

    def chip_factors():
        whole = chip_total[0]
        if chips > 1:
            d_copy(1).wait_recv()
            level_factors(1, lambda d: chip == (0 if d == 0 else 1), whole, chip_total[1])
            whole = whole * chip_total[1]
        chip_total[2] = whole

    def factors(level, d, at):
        return [factor_ref[level, d, i, at, :] for i in range(6)]

    def scan_copy(kind, d, h):
        dst_state = state_ref if d == 0 else end_ref
        src, dst, target = {
            0: lambda: (
                sum_send.at[h, pl.ds(lax.rem(c + 1, cores) * half, half)], core_recv.at[d, h], core_id
            ),
            1: lambda: (chip_send.at[h], chip_recv.at[d, h], chip_id),
            2: lambda: (relay_send.at[h], relay_recv.at[d, h], relay_id(d)),
            3: lambda: (x_start.at[h], chip_start.at[d, h, pl.ds(chip * own, own)], chip_id),
            4: lambda: (core_start.at[h], dst_state.at[h, pl.ds(c * half, half)], core_id),
        }[kind]()
        return remote(src, dst, scan_send.at[kind, d, h], scan_recv.at[kind, d, h], target)

    def send_sums(d, h):
        if cores > 1:
            scan_copy(0, d, h).start()

    def chip_sums(d, h):
        if cores > 1:
            scan_copy(0, d, h).wait_recv()

        def sum_of(j):
            mine_sum = sum_send[h, c * half + j].astype(F32)
            if cores == 1:
                return mine_sum
            f = factors(0, d, pl.ds(h * half + j, 1))
            return f[0] * mine_sum + f[1] * core_recv[d, h, j].astype(F32)

        if chips > 1:
            other = lax.rem(chip + 1, chips)
            for i in range(own):
                chip_send[h, i] = sum_of(other * own + i).astype(BF)
            scan_copy(1, d, h).start()
        for i in range(own):
            chip_own[h, i] = sum_of(chip * own + i)

    def relay(d, h):
        if chips > 1:
            scan_copy(1, d, h).wait_recv()

        @pl.when(first_plane(d))
        def _():
            for i in range(own):
                start = init_ref[i, h].astype(F32) if d == 0 else jnp.zeros((size, size), F32)
                relay_recv[d, h, i] = start

        if planes > 1:
            @pl.when(jnp.logical_not(first_plane(d)))
            def _():
                scan_copy(2, d, h).wait_recv()

        for i in range(own):
            at = pl.ds(h * half + chip * own + i, 1)
            start = relay_recv[d, h, i]
            total = chip_own[h, i]
            here = start
            if chips > 1:
                f = factors(1, d, at)
                away = chip_recv[d, h, i].astype(F32)
                x_start[h, i] = (f[4] * start + f[5] * total).astype(BF)
                here = f[2] * start + f[3] * away
                total = f[0] * total + f[1] * away
            relay_send[h, i] = chip_total[2, at, :] * start + total
            chip_start[d, h, chip * own + i] = here.astype(BF)
        if planes > 1:
            @pl.when(jnp.logical_not(first_plane(1 - d)))
            def _():
                scan_copy(2, d, h).start()
        if chips > 1:
            scan_copy(3, d, h).start()

    def core_states(d, h):
        if chips > 1:
            x_copy = remote(
                x_start.at[h], chip_start.at[d, h, pl.ds(lax.rem(chip + 1, chips) * own, own)],
                scan_send.at[3, d, h], scan_recv.at[3, d, h], chip_id,
            )
            x_copy.wait_recv()
        dst = state_ref if d == 0 else end_ref
        for j in range(half):
            start = chip_start[d, h, j].astype(F32)
            if cores == 1:
                dst[h, j] = start.astype(BF)
                continue
            f = factors(0, d, pl.ds(h * half + j, 1))
            mine_sum = sum_send[h, c * half + j].astype(F32)
            core_start[h, j] = (f[4] * start + f[5] * mine_sum).astype(BF)
            dst[h, c * half + j] = (f[2] * start + f[3] * core_recv[d, h, j].astype(F32)).astype(BF)
        if cores > 1:
            scan_copy(4, d, h).start()

    def wait_states(d, h):
        if cores > 1:
            other = lax.rem(c + 1, cores)
            dst = state_ref if d == 0 else end_ref
            remote(
                core_start.at[h], dst.at[h, pl.ds(other * half, half)],
                scan_send.at[4, d, h], scan_recv.at[4, d, h], core_id,
            ).wait_recv()

    def drain_scan(d):
        for h in range(heads):
            for kind in range(5):
                if kind == 2:
                    if planes > 1:
                        @pl.when(jnp.logical_not(first_plane(1 - d)))
                        def _():
                            scan_copy(kind, d, h).wait_send()
                elif (cores if kind in (0, 4) else chips) > 1:
                    scan_copy(kind, d, h).wait_send()

    def forward_sums(h):
        def body(x):
            key = (k_ref[x, :, cut(h)].astype(F32) * to_end(x, h)).astype(BF)
            sum_send[h, x] = mm_tn(key, v_ref[x, :, cut(h)]).astype(BF)

        each_track(body)
        send_sums(0, h)

    def forward_rows(h):
        wait_states(0, h)

        def body(x):
            q = q_ref[x, :, cut(h)]
            valid = valid_col(x)
            key = (k_ref[x, :, cut(h)].astype(F32) * valid).astype(BF)
            decay = jnp.exp(jnp.where(lower_mask, within(x, h) - row_ref[x, h : h + 1, :], FAR))
            scores = (mm_nt(q, key) * decay).astype(BF)
            outputs = mm(scores, v_ref[x, :, cut(h)]) + from_start(x, h) * mm(q, state_ref[h, x])
            square = jnp.mean(outputs * outputs, axis=-1, keepdims=True)
            inverse = lax.rsqrt(square + EPSILON) * valid
            norm_ref[x, :, cut(h)] = (outputs * inverse).astype(BF)
            out_ref[x, :, cut(h)] = outputs.astype(BF)

        each_track(body)

    def backward_sums(h):
        def body(x):
            outputs = out_ref[x, :, cut(h)].astype(F32)
            square = jnp.mean(outputs * outputs, axis=-1, keepdims=True)
            inverse = lax.rsqrt(square + EPSILON)
            unit = outputs * inverse
            grad = gn_ref[x]
            along = jnp.mean(grad * unit, axis=-1, keepdims=True)
            grad = ((inverse * valid_col(x)) * (grad - unit * along)).astype(BF)
            out_ref[x, :, cut(h)] = grad
            q_from = (q_ref[x, :, cut(h)].astype(F32) * from_start(x, h)).astype(BF)
            sum_send[h, x] = mm_tn(q_from, grad).astype(BF)

        each_track(body)
        send_sums(1, h)

    def backward_rows(h):
        wait_states(1, h)

        def body(x):
            q = q_ref[x, :, cut(h)]
            v = v_ref[x, :, cut(h)]
            valid = valid_col(x)
            key = (k_ref[x, :, cut(h)].astype(F32) * valid).astype(BF)
            grad = out_ref[x, :, cut(h)]
            end_grad = end_ref[h, x]
            decay = jnp.exp(jnp.where(upper_mask, row_ref[x, h : h + 1, :] - within(x, h), FAR))
            grad_scores = (mm_nt(v, grad) * decay).astype(BF)
            scores = (mm_nt(key, q) * decay).astype(BF)
            grad_query = mm_tn(grad_scores, key)
            grad_query = grad_query + from_start(x, h) * mm_nt(grad, state_ref[h, x])
            gq_ref[x, :, cut(h)] = grad_query.astype(BF)
            late = to_end(x, h)
            grad_key = valid * mm(grad_scores, q) + late * mm_nt(v, end_grad)
            gk_ref[x, :, cut(h)] = grad_key.astype(BF)
            grad_value = mm(scores, grad) + late * mm(key, end_grad)
            gv_ref[x, :, cut(h)] = grad_value.astype(BF)

        each_track(body)

    def shared_tables():
        row = lax.broadcasted_iota(jnp.int32, (span, 1), 0)
        lane = lax.broadcasted_iota(jnp.int32, (1, lanes), 1)
        key_length = jnp.zeros((span, 1), jnp.int32)
        for x in range(tracks):
            inside = (row >= x * TILE) & (row < (x + 1) * TILE)
            key_length = jnp.where(inside, len_ref[mine * tracks + x], key_length)
        query_length = jnp.zeros((1, lanes), jnp.int32)
        for s in range(groups):
            group = lax.rem(mine + groups - s, groups)
            for x in range(tracks):
                first = (s * tracks + x) * TILE
                inside = (lane >= first) & (lane < first + TILE)
                query_length = jnp.where(inside, len_ref[group * tracks + x], query_length)
        row_in, lane_in = lax.rem(row, TILE), lax.rem(lane, TILE)
        same = row_in == lane_in
        for tile in range(tiles):
            first = time_first + tile * TILE
            bias_ref[tile] = jnp.where(same & (first + row_in < key_length), 0.0, FAR)
            ratio_ref[2, tile : tile + 1, :] = jnp.where(first + lane_in < query_length, 1.0, 0.0)

    def gather(own_ref, other_ref, at, h):
        pieces = [own_ref[:, at, cut(h)].reshape(span, size)]
        pieces += [other_ref[s, :, at, cut(h)].reshape(span, size) for s in range(groups - 1)]
        return jnp.concatenate(pieces, axis=0)

    def each_tile(body):
        step = 2 if tiles % 2 == 0 else 1

        def run(i, carry):
            for j in range(step):
                tile = i * step + j
                body(tile, pl.ds(pl.multiple_of(tile * TILE, TILE), TILE))
            return carry

        lax.fori_loop(0, tiles // step, run, 0)

    def s_copy(h, s):
        return remote(
            stat_own.at[h], stat_in.at[s - 1, h], s_send.at[h, s - 1], s_recv.at[h, s - 1],
            track_id(s),
        )

    def cross_logits(h):
        for copy in y_copies(h):
            copy.wait_recv()
        slot = h % 2

        def body(tile, at):
            key = ck_ref[:, at, cut(h)].reshape(span, size)
            normed = norm_ref[:, at, cut(h)].reshape(span, size)
            logits = mm_nt(key, gather(cq_ref, qo_ref, at, h)) * scale + bias_ref[tile]
            top = jnp.max(logits, axis=0, keepdims=True)
            e = jnp.exp(logits - top)
            product = mm_nt(normed, gather(g_ref, go_ref, at, h))
            e_ref[slot, tile] = e
            p_ref[slot, tile] = product
            stat_own[h, 0, pl.ds(tile, 1), :] = top
            stat_own[h, 1, pl.ds(tile, 1), :] = jnp.sum(e, axis=0, keepdims=True)
            stat_own[h, 2, pl.ds(tile, 1), :] = jnp.sum(e * product, axis=0, keepdims=True)

        each_tile(body)
        for s in range(1, groups):
            s_copy(h, s).start()

    def p_copy(h, s):
        back = groups - s
        return remote(
            part_send.at[s - 1, :, :, cut(h)], part_recv.at[back - 1, :, :, cut(h)],
            r_send.at[h, s - 1], r_recv.at[h, back - 1],
            {"track": lax.rem(mine + groups - s, groups)},
        )

    def cross_grads(h):
        for s in range(1, groups):
            s_copy(h, s).wait_recv()
        slot = h % 2
        stats = [[stat_own[h, i] for i in range(3)]]
        for s in range(1, groups):
            away = (groups - s) * span
            pieces = [stat_in[s - 1, h, i] for i in range(3)]
            stats.append([jnp.concatenate([a[:, away:], a[:, :away]], axis=1) for a in pieces])
        top = functools.reduce(jnp.maximum, [a[0] for a in stats])
        weights = [jnp.exp(a[0] - top) for a in stats]
        inverse = 1.0 / sum(w * a[1] for w, a in zip(weights, stats))
        ratio_ref[0] = weights[0] * inverse * ratio_ref[2]
        ratio_ref[1] = sum(w * a[2] for w, a in zip(weights, stats)) * inverse

        def body(tile, at):
            key = ck_ref[:, at, cut(h)].reshape(span, size)
            cotangent = gather(g_ref, go_ref, at, h)
            w = e_ref[slot, tile] * ratio_ref[0, pl.ds(tile, 1), :]
            high = w.astype(BF)
            low = (w - high.astype(F32)).astype(BF)
            gn_ref[:, at, :] = (mm(high, cotangent) + mm(low, cotangent)).reshape(
                tracks, TILE, size
            )
            grad = w * ((p_ref[slot, tile] - ratio_ref[1, pl.ds(tile, 1), :]) * scale)
            grad = grad.astype(BF)
            query = gather(cq_ref, qo_ref, at, h)
            gck_ref[:, at, cut(h)] = mm(grad, query).astype(BF).reshape(tracks, TILE, size)
            parts = mm_tn(grad, key)
            own_part[:, at, cut(h)] = parts[:span].reshape(tracks, TILE, size)
            for s in range(1, groups):
                piece = parts[s * span : (s + 1) * span].astype(BF)
                part_send[s - 1, :, at, cut(h)] = piece.reshape(tracks, TILE, size)

        each_tile(body)

    def start_parts(h):
        for s in range(1, groups):
            p_copy(h, s).start()

    def add_parts(h):
        for s in range(1, groups):
            p_copy(h, s).wait_recv()

        def body(x):
            value = own_part[x, :, cut(h)]
            for s in range(groups - 1):
                value = value + part_recv[s, x, :, cut(h)].astype(F32)
            gcq_ref[x, :, cut(h)] = value.astype(BF)

        each_track(body)

    loads[0].wait()
    loads[1].wait()
    core_factors()
    for h in range(heads):
        forward_sums(h)
        if h == 0:
            chip_factors()
        if h >= 1:
            chip_sums(0, h - 1)
    chip_sums(0, heads - 1)
    loads[2].wait()
    loads[3].wait()
    relay(0, 0)
    relay(0, 1)
    shared_tables()
    for i in range(heads + 1):
        if i + 2 < heads:
            relay(0, i + 2)
        if i < heads:
            core_states(0, i)
        if i >= 1:
            forward_rows(i - 1)
        if i == 2:
            start_y(4)
        if i == 6:
            start_y(5)
    for i in (4, 5, 6):
        loads[i].wait()
    drain_scan(0)

    cross_logits(0)
    for i in range(heads + 2):
        if 1 <= i <= heads:
            chip_sums(1, i - 1)
        if i + 1 < heads:
            cross_logits(i + 1)
        if i < heads:
            if i == 1:
                start_y(6)
            if i == 2:
                start_y(7)
            if heads > 8 and i >= 2:
                start_y(i + 6)
            cross_grads(i)
            backward_sums(i)
            if i == heads - 3:
                start_parts(0)
            if i >= heads - 2:
                for h in range(1 if i == heads - 2 else i, i + 1):
                    start_parts(h)
        if i >= 3:
            backward_rows(i - 3)
        if 1 <= i <= heads:
            relay(1, i - 1)
        if i >= 2:
            core_states(1, i - 2)
    for h in range(heads - 1, heads):
        backward_rows(h)
    for h in range(heads):
        add_parts(h)

    drain_scan(1)
    if cores > 1:
        d_copy(0).wait_send()
    if chips > 1:
        d_copy(1).wait_send()
    for h in range(heads):
        for copy in y_copies(h):
            copy.wait_send()
        for s in range(1, groups):
            s_copy(h, s).wait_send()
            p_copy(h, s).wait_send()


def write_kernel(*refs):
    copies = [pltpu.make_async_copy(refs[i], refs[5 + i], refs[10].at[i]) for i in range(5)]
    for copy in copies:
        copy.start()
    for copy in copies:
        copy.wait()


def per_device(
    count,
    groups,
    track_query,
    track_key,
    track_value,
    log_decay,
    valid_length,
    initial_state,
    cross_query,
    cross_key,
    grad_out,
):
    tracks, rows, width = track_query.shape
    heads = log_decay.shape[1]
    size = width // heads
    cores = 2 if tracks % 2 == 0 and count % 2 == 0 else 1
    half = tracks // cores
    chips = 2 if half % 2 == 0 and count % (2 * cores) == 0 else 1
    own = half // chips
    tiles = rows // TILE
    span = tracks * TILE
    lanes = groups * span
    others = max(groups - 1, 1)
    vmem = pl.BlockSpec(memory_space=pltpu.VMEM)
    anywhere = pl.BlockSpec(memory_space=pl.ANY)
    wide = jax.ShapeDtypeStruct((tracks, rows, width), BF)
    block = pltpu.VMEM((tracks, rows, width), BF)
    blocks = pltpu.VMEM((others, tracks, rows, width), BF)
    states = pltpu.VMEM((heads, tracks, size, size), BF)
    dma = pltpu.SemaphoreType.DMA
    dot_flops = 2 * tracks * heads * rows * size * size
    results = pl.pallas_call(
        functools.partial(block_kernel, (groups, count, cores, chips, heads)),
        out_shape=(pltpu.VMEM(wide.shape, BF),) * 5,
        in_specs=[pl.BlockSpec(memory_space=pltpu.SMEM), vmem] + [anywhere] * 7,
        out_specs=(vmem,) * 5,
        scratch_shapes=[block] * 6
        + [pltpu.VMEM((own, heads, size, size), BF)]
        + [blocks] * 4
        + [pltpu.VMEM((tracks, rows, width), F32), block, block, states, states]
        + [
            states,
            pltpu.VMEM((2, heads, half, size, size), BF),
            pltpu.VMEM((heads, own, size, size), BF),
            pltpu.VMEM((heads, own, size, size), F32),
            pltpu.VMEM((2, heads, own, size, size), BF),
            pltpu.VMEM((heads, own, size, size), F32),
            pltpu.VMEM((2, heads, own, size, size), F32),
            pltpu.VMEM((heads, own, size, size), BF),
            pltpu.VMEM((2, heads, half, size, size), BF),
            pltpu.VMEM((heads, half, size, size), BF),
            pltpu.VMEM((2, tiles, span, lanes), F32),
            pltpu.VMEM((2, tiles, span, lanes), F32),
            pltpu.VMEM((tiles, span, lanes), F32),
            pltpu.VMEM((tracks, rows, size), F32),
            pltpu.VMEM((tracks, rows, 128), F32),
            pltpu.VMEM((tracks, heads, rows), F32),
            pltpu.VMEM((3, tiles, lanes), F32),
            pltpu.VMEM((heads, 3, tiles, lanes), F32),
            pltpu.VMEM((others, heads, 3, tiles, lanes), F32),
            pltpu.VMEM((cores, heads * half, 128), F32),
            pltpu.VMEM((heads * half, 128), F32),
            pltpu.VMEM((3, heads * half, 128), F32),
            pltpu.VMEM((2, 2, 6, heads * half, 128), F32),
            dma((7,)),
            dma((2, heads, others)),
            dma((2, heads, others)),
        ]
        + [dma((heads, others))] * 4
        + [dma((5, 2, heads))] * 2
        + [dma((2,))] * 2,
        compiler_params=pltpu.CompilerParams(
            collective_id=0, has_side_effects=True, vmem_limit_bytes=VMEM_BYTES - 5 * wide.size * 2
        ),
        cost_estimate=pl.CostEstimate(
            flops=20 * dot_flops, bytes_accessed=24 * tracks * rows * width, transcendentals=0
        ),
        name="block_backward",
    )(
        valid_length, log_decay, track_query, track_key, track_value, initial_state,
        cross_query, cross_key, grad_out,
    )
    return pl.pallas_call(
        write_kernel,
        out_shape=(wide,) * 5,
        in_specs=[vmem] * 5,
        out_specs=(anywhere,) * 5,
        scratch_shapes=[dma((5,))],
        compiler_params=pltpu.CompilerParams(vmem_limit_bytes=2**20),
        name="write_results",
    )(*results)


def solution(mesh):
    wide = P("track", "tm", None)
    return jax.shard_map(
        functools.partial(per_device, mesh.shape["tm"], mesh.shape["track"]),
        mesh=mesh,
        in_specs=(
            wide,
            wide,
            wide,
            P("track", None, "tm"),
            P(),
            P("track", None, None, None),
            wide,
            wide,
            wide,
        ),
        out_specs=(wide,) * 5,
        check_vma=False,
    )
```

```python
import functools

import jax
import jax.numpy as jnp
from jax import lax
from jax.experimental import pallas as pl
from jax.experimental.pallas import tpu as pltpu
from jax.sharding import PartitionSpec as P

EPSILON = 1e-06
MESH = pl.DeviceIdType.MESH
BF = jnp.bfloat16
F32 = jnp.float32
TILE = 16
VMEM_BYTES = 67043328
FAR = -1e30


def mm(a, b):
    return lax.dot_general(a, b, (((1,), (0,)), ((), ())), preferred_element_type=F32)


def mm_nt(a, b):
    return lax.dot_general(a, b, (((1,), (1,)), ((), ())), preferred_element_type=F32)


def mm_tn(a, b):
    return lax.dot_general(a, b, (((0,), (0,)), ((), ())), preferred_element_type=F32)


def remote(src, dst, send_sem, recv_sem, target):
    return pltpu.make_async_remote_copy(
        src_ref=src, dst_ref=dst, send_sem=send_sem, recv_sem=recv_sem,
        device_id=target, device_id_type=MESH,
    )


def split3(x):
    a = x.astype(BF)
    rest = x - a.astype(F32)
    b = rest.astype(BF)
    return a, b, (rest - b.astype(F32)).astype(BF)


def block_kernel(
    dims, len_ref, decay_ref, q_hbm, k_hbm, v_hbm, init_hbm, cq_hbm, ck_hbm, g_hbm,
    gq_ref, gk_ref, gv_ref, gcq_ref, gck_ref,
    q_ref, k_ref, v_ref, cq_ref, ck_ref, g_ref, init_ref,
    qo_ref, go_ref, part_send, part_recv, own_part,
    out_ref, norm_ref, state_ref, end_ref,
    sum_send, core_recv, chip_send, chip_own, chip_recv, relay_send, relay_recv,
    x_start, chip_start, core_start,
    e_ref, p_ref, bias_ref, gn_ref, col_ref, row_ref, ratio_ref,
    stat_own, stat_in, total_ref, core_total, chip_total, factor_ref,
    in_sem, y_send, y_recv, s_send, s_recv, r_send, r_recv, scan_send, scan_recv, d_send, d_recv,
):
    groups, count, cores, chips, heads = dims
    planes = count // (cores * chips)
    tracks, rows, width = q_ref.shape
    size = width // heads
    half = tracks // cores
    own = half // chips
    tiles = rows // TILE
    span = tracks * TILE
    lanes = groups * span
    scale = 1.0 / float(size) ** 0.5
    pair = 2 if tracks % 2 == 0 else 1

    me = lax.axis_index("tm")
    mine = lax.axis_index("track")
    c = lax.rem(me, cores)
    chip = lax.rem(me // cores, chips)
    z = me // (cores * chips)
    mine_first = c * half + chip * own
    time_first = me * rows

    def cut(h):
        return slice(h * size, (h + 1) * size)

    def place(plane, column, core):
        return {"tm": (plane * chips + column) * cores + core}

    core_id = place(z, chip, lax.rem(c + 1, cores))
    chip_id = place(z, lax.rem(chip + 1, chips), c)

    def relay_id(d):
        return place(lax.rem(z + (1 if d == 0 else planes - 1), planes), chip, c)

    def first_plane(d):
        return z == (0 if d == 0 else planes - 1)

    def track_id(s):
        return {"track": lax.rem(mine + s, groups)}

    hbm = (k_hbm, v_hbm, q_hbm, init_hbm.at[pl.ds(mine_first, own)], ck_hbm, cq_hbm, g_hbm)
    vmem = (k_ref, v_ref, q_ref, init_ref, ck_ref, cq_ref, g_ref)
    loads = [pltpu.make_async_copy(a, b, in_sem.at[i]) for i, (a, b) in enumerate(zip(hbm, vmem))]
    for load in loads:
        load.start()

    barrier = pltpu.get_barrier_semaphore()
    peers = [track_id(s) for s in range(1, groups)]
    if cores > 1:
        peers.append(core_id)
    if chips > 1:
        peers.append(chip_id)
    for peer in peers:
        pl.semaphore_signal(barrier, inc=1, device_id=peer, device_id_type=MESH)
    for d in range(2):
        @pl.when(jnp.logical_not(first_plane(1 - d)))
        def _():
            pl.semaphore_signal(barrier, inc=1, device_id=relay_id(d), device_id_type=MESH)
    inner = jnp.where(first_plane(0), 0, 1) + jnp.where(first_plane(1), 0, 1)
    pl.semaphore_wait(barrier, len(peers) + inner)

    def y_copies(h):
        return [
            remote(
                src.at[:, :, cut(h)], dst.at[s - 1, :, :, cut(h)],
                y_send.at[kind, h, s - 1], y_recv.at[kind, h, s - 1], track_id(s),
            )
            for s in range(1, groups)
            for kind, (src, dst) in enumerate(((cq_hbm, qo_ref), (g_hbm, go_ref)))
        ]

    def start_y(h):
        if h < heads:
            for copy in y_copies(h):
                copy.start()

    for h in range(4):
        start_y(h)

    t_index = lax.broadcasted_iota(jnp.int32, (rows, rows), 0)
    s_index = lax.broadcasted_iota(jnp.int32, (rows, rows), 1)
    lower_mask = t_index >= s_index
    upper_mask = t_index <= s_index
    lower = jnp.where(lower_mask, 1.0, 0.0).astype(BF)
    upper = jnp.where(upper_mask, 1.0, 0.0).astype(BF)
    row_time = time_first + lax.broadcasted_iota(jnp.int32, (rows, 1), 0)

    for x in range(tracks):
        parts = split3(decay_ref[x])
        col = sum(mm_nt(lower, part) for part in parts)
        row = sum(mm(part, upper) for part in parts)
        valid = jnp.where(row_time < len_ref[mine * tracks + x], 1.0, 0.0)
        col_ref[x, :, 0:heads] = col
        col_ref[x, :, heads : 2 * heads] = jnp.exp(col)
        col_ref[x, :, 2 * heads : 3 * heads] = jnp.exp(col[rows - 1 : rows, :] - col) * valid
        col_ref[x, :, 3 * heads : 3 * heads + 1] = valid
        row_ref[x] = row
        total = jnp.broadcast_to(jnp.exp(row[:, rows - 1 : rows]), (heads, 128))
        for h in range(heads):
            at = h * half + x % half
            total_ref[x // half, at : at + 1, :] = total[h : h + 1]

    def d_copy(level):
        if level == 0:
            other = lax.rem(c + 1, cores)
            return remote(total_ref.at[other], core_total, d_send.at[0], d_recv.at[0], core_id)
        return remote(chip_total.at[0], chip_total.at[1], d_send.at[1], d_recv.at[1], chip_id)

    if cores > 1:
        d_copy(0).start()

    def within(x, h):
        return col_ref[x, :, h : h + 1]

    def from_start(x, h):
        return col_ref[x, :, heads + h : heads + h + 1]

    def to_end(x, h):
        return col_ref[x, :, 2 * heads + h : 2 * heads + h + 1]

    def valid_col(x):
        return col_ref[x, :, 3 * heads : 3 * heads + 1]

    def each_track(body, step=pair):
        def run(i, carry):
            for j in range(step):
                body(i * step + j)
            return carry

        lax.fori_loop(0, tracks // step, run, 0)

    def level_factors(level, earlier, own_decay, other_decay):
        for d in range(2):
            first = earlier(d)
            one, none = jnp.ones_like(own_decay), jnp.zeros_like(own_decay)
            factor_ref[level, d, 0] = jnp.where(first, other_decay, one)
            factor_ref[level, d, 1] = jnp.where(first, one, own_decay)
            factor_ref[level, d, 2] = jnp.where(first, one, other_decay)
            factor_ref[level, d, 3] = jnp.where(first, none, one)
            factor_ref[level, d, 4] = jnp.where(first, own_decay, one)
            factor_ref[level, d, 5] = jnp.where(first, one, none)

    def core_factors():
        own_decay = total_ref[c]
        whole = own_decay
        if cores > 1:
            d_copy(0).wait_recv()
            other_decay = core_total[...]
            whole = own_decay * other_decay
            level_factors(0, lambda d: c == (0 if d == 0 else 1), own_decay, other_decay)
        chip_total[0] = whole
        if chips > 1:
            d_copy(1).start()

    def chip_factors():
        whole = chip_total[0]
        if chips > 1:
            d_copy(1).wait_recv()
            level_factors(1, lambda d: chip == (0 if d == 0 else 1), whole, chip_total[1])
            whole = whole * chip_total[1]
        chip_total[2] = whole

    def factors(level, d, at):
        return [factor_ref[level, d, i, at, :] for i in range(6)]

    def scan_copy(kind, d, h):
        dst_state = state_ref if d == 0 else end_ref
        src, dst, target = {
            0: lambda: (
                sum_send.at[h, pl.ds(lax.rem(c + 1, cores) * half, half)], core_recv.at[d, h], core_id
            ),
            1: lambda: (chip_send.at[h], chip_recv.at[d, h], chip_id),
            2: lambda: (relay_send.at[h], relay_recv.at[d, h], relay_id(d)),
            3: lambda: (x_start.at[h], chip_start.at[d, h, pl.ds(chip * own, own)], chip_id),
            4: lambda: (core_start.at[h], dst_state.at[h, pl.ds(c * half, half)], core_id),
        }[kind]()
        return remote(src, dst, scan_send.at[kind, d, h], scan_recv.at[kind, d, h], target)

    def send_sums(d, h):
        if cores > 1:
            scan_copy(0, d, h).start()

    def chip_sums(d, h):
        if cores > 1:
            scan_copy(0, d, h).wait_recv()

        def sum_of(j):
            mine_sum = sum_send[h, c * half + j].astype(F32)
            if cores == 1:
                return mine_sum
            f = factors(0, d, pl.ds(h * half + j, 1))
            return f[0] * mine_sum + f[1] * core_recv[d, h, j].astype(F32)

        if chips > 1:
            other = lax.rem(chip + 1, chips)
            for i in range(own):
                chip_send[h, i] = sum_of(other * own + i).astype(BF)
            scan_copy(1, d, h).start()
        for i in range(own):
            chip_own[h, i] = sum_of(chip * own + i)

    def relay(d, h):
        if chips > 1:
            scan_copy(1, d, h).wait_recv()

        @pl.when(first_plane(d))
        def _():
            for i in range(own):
                start = init_ref[i, h].astype(F32) if d == 0 else jnp.zeros((size, size), F32)
                relay_recv[d, h, i] = start

        if planes > 1:
            @pl.when(jnp.logical_not(first_plane(d)))
            def _():
                scan_copy(2, d, h).wait_recv()

        for i in range(own):
            at = pl.ds(h * half + chip * own + i, 1)
            start = relay_recv[d, h, i]
            total = chip_own[h, i]
            here = start
            if chips > 1:
                f = factors(1, d, at)
                away = chip_recv[d, h, i].astype(F32)
                x_start[h, i] = (f[4] * start + f[5] * total).astype(BF)
                here = f[2] * start + f[3] * away
                total = f[0] * total + f[1] * away
            relay_send[h, i] = chip_total[2, at, :] * start + total
            chip_start[d, h, chip * own + i] = here.astype(BF)
        if planes > 1:
            @pl.when(jnp.logical_not(first_plane(1 - d)))
            def _():
                scan_copy(2, d, h).start()
        if chips > 1:
            scan_copy(3, d, h).start()

    def core_states(d, h):
        if chips > 1:
            x_copy = remote(
                x_start.at[h], chip_start.at[d, h, pl.ds(lax.rem(chip + 1, chips) * own, own)],
                scan_send.at[3, d, h], scan_recv.at[3, d, h], chip_id,
            )
            x_copy.wait_recv()
        dst = state_ref if d == 0 else end_ref
        for j in range(half):
            start = chip_start[d, h, j].astype(F32)
            if cores == 1:
                dst[h, j] = start.astype(BF)
                continue
            f = factors(0, d, pl.ds(h * half + j, 1))
            mine_sum = sum_send[h, c * half + j].astype(F32)
            core_start[h, j] = (f[4] * start + f[5] * mine_sum).astype(BF)
            dst[h, c * half + j] = (f[2] * start + f[3] * core_recv[d, h, j].astype(F32)).astype(BF)
        if cores > 1:
            scan_copy(4, d, h).start()

    def wait_states(d, h):
        if cores > 1:
            other = lax.rem(c + 1, cores)
            dst = state_ref if d == 0 else end_ref
            remote(
                core_start.at[h], dst.at[h, pl.ds(other * half, half)],
                scan_send.at[4, d, h], scan_recv.at[4, d, h], core_id,
            ).wait_recv()

    def drain_scan(d):
        for h in range(heads):
            for kind in range(5):
                if kind == 2:
                    if planes > 1:
                        @pl.when(jnp.logical_not(first_plane(1 - d)))
                        def _():
                            scan_copy(kind, d, h).wait_send()
                elif (cores if kind in (0, 4) else chips) > 1:
                    scan_copy(kind, d, h).wait_send()

    def forward_sums(h):
        def body(x):
            key = (k_ref[x, :, cut(h)].astype(F32) * to_end(x, h)).astype(BF)
            sum_send[h, x] = mm_tn(key, v_ref[x, :, cut(h)]).astype(BF)

        each_track(body)
        send_sums(0, h)

    def forward_rows(h):
        wait_states(0, h)

        def body(x):
            q = q_ref[x, :, cut(h)]
            valid = valid_col(x)
            key = (k_ref[x, :, cut(h)].astype(F32) * valid).astype(BF)
            decay = jnp.exp(jnp.where(lower_mask, within(x, h) - row_ref[x, h : h + 1, :], FAR))
            scores = (mm_nt(q, key) * decay).astype(BF)
            outputs = mm(scores, v_ref[x, :, cut(h)]) + from_start(x, h) * mm(q, state_ref[h, x])
            square = jnp.mean(outputs * outputs, axis=-1, keepdims=True)
            inverse = lax.rsqrt(square + EPSILON) * valid
            norm_ref[x, :, cut(h)] = (outputs * inverse).astype(BF)
            out_ref[x, :, cut(h)] = outputs.astype(BF)

        each_track(body)

    def backward_sums(h):
        def body(x):
            outputs = out_ref[x, :, cut(h)].astype(F32)
            square = jnp.mean(outputs * outputs, axis=-1, keepdims=True)
            inverse = lax.rsqrt(square + EPSILON)
            unit = outputs * inverse
            grad = gn_ref[x]
            along = jnp.mean(grad * unit, axis=-1, keepdims=True)
            grad = ((inverse * valid_col(x)) * (grad - unit * along)).astype(BF)
            out_ref[x, :, cut(h)] = grad
            q_from = (q_ref[x, :, cut(h)].astype(F32) * from_start(x, h)).astype(BF)
            sum_send[h, x] = mm_tn(q_from, grad).astype(BF)

        each_track(body)
        send_sums(1, h)

    def backward_rows(h):
        wait_states(1, h)

        def body(x):
            q = q_ref[x, :, cut(h)]
            v = v_ref[x, :, cut(h)]
            valid = valid_col(x)
            key = (k_ref[x, :, cut(h)].astype(F32) * valid).astype(BF)
            grad = out_ref[x, :, cut(h)]
            end_grad = end_ref[h, x]
            decay = jnp.exp(jnp.where(upper_mask, row_ref[x, h : h + 1, :] - within(x, h), FAR))
            grad_scores = (mm_nt(v, grad) * decay).astype(BF)
            scores = (mm_nt(key, q) * decay).astype(BF)
            grad_query = mm_tn(grad_scores, key)
            grad_query = grad_query + from_start(x, h) * mm_nt(grad, state_ref[h, x])
            gq_ref[x, :, cut(h)] = grad_query.astype(BF)
            late = to_end(x, h)
            grad_key = valid * mm(grad_scores, q) + late * mm_nt(v, end_grad)
            gk_ref[x, :, cut(h)] = grad_key.astype(BF)
            grad_value = mm(scores, grad) + late * mm(key, end_grad)
            gv_ref[x, :, cut(h)] = grad_value.astype(BF)

        each_track(body)

    def shared_tables():
        row = lax.broadcasted_iota(jnp.int32, (span, 1), 0)
        lane = lax.broadcasted_iota(jnp.int32, (1, lanes), 1)
        key_length = jnp.zeros((span, 1), jnp.int32)
        for x in range(tracks):
            inside = (row >= x * TILE) & (row < (x + 1) * TILE)
            key_length = jnp.where(inside, len_ref[mine * tracks + x], key_length)
        query_length = jnp.zeros((1, lanes), jnp.int32)
        for s in range(groups):
            group = lax.rem(mine + groups - s, groups)
            for x in range(tracks):
                first = (s * tracks + x) * TILE
                inside = (lane >= first) & (lane < first + TILE)
                query_length = jnp.where(inside, len_ref[group * tracks + x], query_length)
        row_in, lane_in = lax.rem(row, TILE), lax.rem(lane, TILE)
        same = row_in == lane_in
        for tile in range(tiles):
            first = time_first + tile * TILE
            bias_ref[tile] = jnp.where(same & (first + row_in < key_length), 0.0, FAR)
            ratio_ref[2, tile : tile + 1, :] = jnp.where(first + lane_in < query_length, 1.0, 0.0)

    def gather(own_ref, other_ref, at, h):
        pieces = [own_ref[:, at, cut(h)].reshape(span, size)]
        pieces += [other_ref[s, :, at, cut(h)].reshape(span, size) for s in range(groups - 1)]
        return jnp.concatenate(pieces, axis=0)

    def each_tile(body):
        step = 2 if tiles % 2 == 0 else 1

        def run(i, carry):
            for j in range(step):
                tile = i * step + j
                body(tile, pl.ds(pl.multiple_of(tile * TILE, TILE), TILE))
            return carry

        lax.fori_loop(0, tiles // step, run, 0)

    def s_copy(h, s):
        return remote(
            stat_own.at[h], stat_in.at[s - 1, h], s_send.at[h, s - 1], s_recv.at[h, s - 1],
            track_id(s),
        )

    def cross_logits(h):
        for copy in y_copies(h):
            copy.wait_recv()
        slot = h % 2

        def body(tile, at):
            key = ck_ref[:, at, cut(h)].reshape(span, size)
            normed = norm_ref[:, at, cut(h)].reshape(span, size)
            logits = mm_nt(key, gather(cq_ref, qo_ref, at, h)) * scale + bias_ref[tile]
            top = jnp.max(logits, axis=0, keepdims=True)
            e = jnp.exp(logits - top)
            product = mm_nt(normed, gather(g_ref, go_ref, at, h))
            e_ref[slot, tile] = e
            p_ref[slot, tile] = product
            stat_own[h, 0, pl.ds(tile, 1), :] = top
            stat_own[h, 1, pl.ds(tile, 1), :] = jnp.sum(e, axis=0, keepdims=True)
            stat_own[h, 2, pl.ds(tile, 1), :] = jnp.sum(e * product, axis=0, keepdims=True)

        each_tile(body)
        for s in range(1, groups):
            s_copy(h, s).start()

    def p_copy(h, s):
        back = groups - s
        return remote(
            part_send.at[s - 1, :, :, cut(h)], part_recv.at[back - 1, :, :, cut(h)],
            r_send.at[h, s - 1], r_recv.at[h, back - 1],
            {"track": lax.rem(mine + groups - s, groups)},
        )

    def cross_grads(h):
        for s in range(1, groups):
            s_copy(h, s).wait_recv()
        slot = h % 2
        stats = [[stat_own[h, i] for i in range(3)]]
        for s in range(1, groups):
            away = (groups - s) * span
            pieces = [stat_in[s - 1, h, i] for i in range(3)]
            stats.append([jnp.concatenate([a[:, away:], a[:, :away]], axis=1) for a in pieces])
        top = functools.reduce(jnp.maximum, [a[0] for a in stats])
        weights = [jnp.exp(a[0] - top) for a in stats]
        inverse = 1.0 / sum(w * a[1] for w, a in zip(weights, stats))
        ratio_ref[0] = weights[0] * inverse * ratio_ref[2]
        ratio_ref[1] = sum(w * a[2] for w, a in zip(weights, stats)) * inverse

        def body(tile, at):
            key = ck_ref[:, at, cut(h)].reshape(span, size)
            cotangent = gather(g_ref, go_ref, at, h)
            w = e_ref[slot, tile] * ratio_ref[0, pl.ds(tile, 1), :]
            high = w.astype(BF)
            low = (w - high.astype(F32)).astype(BF)
            gn_ref[:, at, :] = (mm(high, cotangent) + mm(low, cotangent)).reshape(
                tracks, TILE, size
            )
            grad = w * ((p_ref[slot, tile] - ratio_ref[1, pl.ds(tile, 1), :]) * scale)
            grad = grad.astype(BF)
            query = gather(cq_ref, qo_ref, at, h)
            gck_ref[:, at, cut(h)] = mm(grad, query).astype(BF).reshape(tracks, TILE, size)
            parts = mm_tn(grad, key)
            own_part[:, at, cut(h)] = parts[:span].reshape(tracks, TILE, size)
            for s in range(1, groups):
                piece = parts[s * span : (s + 1) * span].astype(BF)
                part_send[s - 1, :, at, cut(h)] = piece.reshape(tracks, TILE, size)

        each_tile(body)

    def start_parts(h):
        for s in range(1, groups):
            p_copy(h, s).start()

    def add_parts(h):
        for s in range(1, groups):
            p_copy(h, s).wait_recv()

        def body(x):
            value = own_part[x, :, cut(h)]
            for s in range(groups - 1):
                value = value + part_recv[s, x, :, cut(h)].astype(F32)
            gcq_ref[x, :, cut(h)] = value.astype(BF)

        each_track(body)

    loads[0].wait()
    loads[1].wait()
    core_factors()
    for h in range(heads):
        forward_sums(h)
        if h == 0:
            chip_factors()
        if h >= 1:
            chip_sums(0, h - 1)
    chip_sums(0, heads - 1)
    loads[2].wait()
    loads[3].wait()
    relay(0, 0)
    relay(0, 1)
    shared_tables()
    for i in range(heads + 1):
        if i + 2 < heads:
            relay(0, i + 2)
        if i < heads:
            core_states(0, i)
        if i >= 1:
            forward_rows(i - 1)
        if i == 2:
            start_y(4)
        if i == 6:
            start_y(5)
    for i in (4, 5, 6):
        loads[i].wait()
    drain_scan(0)

    cross_logits(0)
    lag = planes - 1
    sent = 0
    for i in range(heads + lag + 3):
        if 1 <= i <= heads:
            chip_sums(1, i - 1)
        if i + 1 < heads:
            cross_logits(i + 1)
        if i < heads:
            if i == 0:
                start_y(6)
            if i == 2:
                start_y(7)
            if heads > 8 and i >= 2:
                start_y(i + 6)
            cross_grads(i)
            ready = {3: 1, 2: 2, 1: 4, 0: heads - 1}.get(heads - 2 - i, 0) if i < heads - 1 else heads
            ready = min(ready, i + 1)
            while sent < ready:
                start_parts(sent)
                sent += 1
            backward_sums(i)
        if 0 <= i - lag - 3:
            backward_rows(i - lag - 3)
        if 1 <= i <= heads + lag:
            h = i - 1 - (lag - z)

            @pl.when((h >= 0) & (h < heads))
            def _():
                relay(1, h)
        if 0 <= i - lag - 2 < heads:
            core_states(1, i - lag - 2)
    for h in range(heads):
        add_parts(h)

    drain_scan(1)
    if cores > 1:
        d_copy(0).wait_send()
    if chips > 1:
        d_copy(1).wait_send()
    for h in range(heads):
        for copy in y_copies(h):
            copy.wait_send()
        for s in range(1, groups):
            s_copy(h, s).wait_send()
            p_copy(h, s).wait_send()


def write_kernel(*refs):
    copies = [pltpu.make_async_copy(refs[i], refs[5 + i], refs[10].at[i]) for i in range(5)]
    for copy in copies:
        copy.start()
    for copy in copies:
        copy.wait()


def per_device(
    count,
    groups,
    track_query,
    track_key,
    track_value,
    log_decay,
    valid_length,
    initial_state,
    cross_query,
    cross_key,
    grad_out,
):
    tracks, rows, width = track_query.shape
    heads = log_decay.shape[1]
    size = width // heads
    cores = 2 if tracks % 2 == 0 and count % 2 == 0 else 1
    half = tracks // cores
    chips = 2 if half % 2 == 0 and count % (2 * cores) == 0 else 1
    own = half // chips
    tiles = rows // TILE
    span = tracks * TILE
    lanes = groups * span
    others = max(groups - 1, 1)
    vmem = pl.BlockSpec(memory_space=pltpu.VMEM)
    anywhere = pl.BlockSpec(memory_space=pl.ANY)
    wide = jax.ShapeDtypeStruct((tracks, rows, width), BF)
    block = pltpu.VMEM((tracks, rows, width), BF)
    blocks = pltpu.VMEM((others, tracks, rows, width), BF)
    states = pltpu.VMEM((heads, tracks, size, size), BF)
    dma = pltpu.SemaphoreType.DMA
    dot_flops = 2 * tracks * heads * rows * size * size
    results = pl.pallas_call(
        functools.partial(block_kernel, (groups, count, cores, chips, heads)),
        out_shape=(pltpu.VMEM(wide.shape, BF),) * 5,
        in_specs=[pl.BlockSpec(memory_space=pltpu.SMEM), vmem] + [anywhere] * 7,
        out_specs=(vmem,) * 5,
        scratch_shapes=[block] * 6
        + [pltpu.VMEM((own, heads, size, size), BF)]
        + [blocks] * 4
        + [pltpu.VMEM((tracks, rows, width), F32), block, block, states, states]
        + [
            states,
            pltpu.VMEM((2, heads, half, size, size), BF),
            pltpu.VMEM((heads, own, size, size), BF),
            pltpu.VMEM((heads, own, size, size), F32),
            pltpu.VMEM((2, heads, own, size, size), BF),
            pltpu.VMEM((heads, own, size, size), F32),
            pltpu.VMEM((2, heads, own, size, size), F32),
            pltpu.VMEM((heads, own, size, size), BF),
            pltpu.VMEM((2, heads, half, size, size), BF),
            pltpu.VMEM((heads, half, size, size), BF),
            pltpu.VMEM((2, tiles, span, lanes), F32),
            pltpu.VMEM((2, tiles, span, lanes), F32),
            pltpu.VMEM((tiles, span, lanes), F32),
            pltpu.VMEM((tracks, rows, size), F32),
            pltpu.VMEM((tracks, rows, 128), F32),
            pltpu.VMEM((tracks, heads, rows), F32),
            pltpu.VMEM((3, tiles, lanes), F32),
            pltpu.VMEM((heads, 3, tiles, lanes), F32),
            pltpu.VMEM((others, heads, 3, tiles, lanes), F32),
            pltpu.VMEM((cores, heads * half, 128), F32),
            pltpu.VMEM((heads * half, 128), F32),
            pltpu.VMEM((3, heads * half, 128), F32),
            pltpu.VMEM((2, 2, 6, heads * half, 128), F32),
            dma((7,)),
            dma((2, heads, others)),
            dma((2, heads, others)),
        ]
        + [dma((heads, others))] * 4
        + [dma((5, 2, heads))] * 2
        + [dma((2,))] * 2,
        compiler_params=pltpu.CompilerParams(
            collective_id=0, has_side_effects=True, vmem_limit_bytes=VMEM_BYTES - 5 * wide.size * 2
        ),
        cost_estimate=pl.CostEstimate(
            flops=20 * dot_flops, bytes_accessed=24 * tracks * rows * width, transcendentals=0
        ),
        name="block_backward",
    )(
        valid_length, log_decay, track_query, track_key, track_value, initial_state,
        cross_query, cross_key, grad_out,
    )
    return pl.pallas_call(
        write_kernel,
        out_shape=(wide,) * 5,
        in_specs=[vmem] * 5,
        out_specs=(anywhere,) * 5,
        scratch_shapes=[dma((5,))],
        compiler_params=pltpu.CompilerParams(vmem_limit_bytes=2**20),
        name="write_results",
    )(*results)


def solution(mesh):
    wide = P("track", "tm", None)
    return jax.shard_map(
        functools.partial(per_device, mesh.shape["tm"], mesh.shape["track"]),
        mesh=mesh,
        in_specs=(
            wide,
            wide,
            wide,
            P("track", None, "tm"),
            P(),
            P("track", None, None, None),
            wide,
            wide,
            wide,
        ),
        out_specs=(wide,) * 5,
        check_vma=False,
    )
```
